32 devices in a mesh: gx: 2 (over x), gy: 8 (over z, core), gz: 2 (over y).
Axes of the slice: x: 2, y: 2, z: 4, core: 2. Of those that a mesh axis runs over, the one named last changes fastest.
Arguments:
- state_field: float32 [32, 64, 32, 256], P('gx', 'gy', 'gz'), may hold values from -6 to 6
- norm_gains: float32 [4, 256], replicated, may hold values from 0.1 to 1.9
- project_in: bfloat16 [3, 256, 768], replicated, may hold values from -24 to 24
- project_out: bfloat16 [3, 256, 256], replicated, may hold values from -0.375 to 0.375
- expand_weight: bfloat16 [256, 1024], replicated, may hold values from -0.375 to 0.375
- reduce_weight: bfloat16 [1024, 256], replicated, may hold values from -0.1875 to 0.1875
Outputs:
- block_out: float32 [32, 64, 32, 256], P('gx', 'gy', 'gz')
The draws below stay inside these ranges and needn't reach their ends.
All inputs are finite; a program needn't handle non-finite values.
Results may differ from the reference program's by a relative error of at most 0.039.
Values may be sent and summed in bfloat16 or wider, within the bound.
No kernel may reach another device: no remote copies, remote signals or barrier semaphores. Data moves between devices by JAX's collectives and lax.ppermute only.
A program may use at most 128 MiB of HBM per device.

```python
import jax
import jax.numpy as jnp
from jax import lax

WIDTH = 256
HEADS = 8
HEAD_DIM = 32
FFN_WIDTH = 1024
GRID_X = 32
GRID_Y = 64
GRID_Z = 32


def draw_project_in(key, part):
    base = jax.random.normal(key, (3, WIDTH, 3 * WIDTH), jnp.float32) * WIDTH ** (-0.5)
    return base.astype(jnp.bfloat16)


def block_levels(stream_key, extent, shards, least, largest):
    factor_of, own = 1.0, jax.random.fold_in(stream_key, 6)
    for axis_at, blocks in shards:
        steps = jnp.exp(jax.random.uniform(jax.random.fold_in(own, axis_at), (blocks,), jnp.float32, least / len(shards), largest / len(shards)))
        factor_of = factor_of * jnp.repeat(steps, extent[axis_at] // blocks).reshape([-1 if axis == axis_at else 1 for axis in range(len(extent))])
    return factor_of


def centred(own_key, shape, width, reach, pieces=(), kind=jnp.bfloat16):
    array = width * jax.random.normal(own_key, shape, jnp.float32)
    if pieces:
        array = array * block_levels(own_key, shape, pieces, -0.22, 0.18)
    return jnp.clip(array, -reach, reach).astype(kind)


def setup_inputs(seed: int = 0) -> dict:
    keys = jax.random.split(jax.random.key(seed), 7)
    return {
        "state_field": centred(keys[0], (GRID_X, GRID_Y, GRID_Z, WIDTH), 1.0, 6.0, ((0, 2), (1, 8), (2, 2)), jnp.float32),
        "norm_gains": jnp.clip(1.0 + 0.18 * jax.random.normal(keys[1], (4, WIDTH), jnp.float32), 0.1, 1.9),
        "project_in": draw_project_in(jax.random.fold_in(keys[6], 71), 0),
        "project_out": centred(keys[3], (3, WIDTH, WIDTH), WIDTH ** -0.5, 0.375),
        "expand_weight": centred(keys[4], (WIDTH, FFN_WIDTH), WIDTH ** -0.5, 0.375),
        "reduce_weight": centred(keys[5], (FFN_WIDTH, WIDTH), FFN_WIDTH ** -0.5, 0.1875),
    }


def layer_norm(inputs, gain_row):
    center = inputs - lax.optimization_barrier(jnp.mean(inputs, axis=-1, keepdims=True))
    spread = lax.optimization_barrier(jnp.mean(center * center, axis=-1, keepdims=True))
    return (center * lax.rsqrt(spread + 1e-05) * gain_row).astype(jnp.bfloat16)

def sweep_slab(slab, gain_row, weight_in, weight_out):
    normed = layer_norm(slab, gain_row)
    count = slab.shape[0]
    length = slab.shape[1]
    packed = jnp.dot(normed.reshape(-1, WIDTH), weight_in, preferred_element_type=jnp.float32).astype(jnp.bfloat16)
    packed = packed.reshape(count, length, 3, HEADS, HEAD_DIM).astype(jnp.float32)
    scores = jnp.einsum('plhd,pmhd->phlm', packed[:, :, 0], packed[:, :, 1]) * HEAD_DIM ** (-0.5)
    peak = lax.optimization_barrier(jnp.max(scores, axis=-1, keepdims=True))
    expo = jnp.exp(scores - peak)
    weights = (expo / lax.optimization_barrier(jnp.sum(expo, axis=-1, keepdims=True))).astype(jnp.bfloat16)
    mixed = jnp.einsum('phlm,pmhd->plhd', weights.astype(jnp.float32), packed[:, :, 2]).astype(jnp.bfloat16)
    update = jnp.dot(mixed.reshape(-1, WIDTH), weight_out, preferred_element_type=jnp.float32)
    return slab + update.reshape(slab.shape)

def reference(state_field, norm_gains, project_in, project_out, expand_weight, reduce_weight):

    def sweep_first(slab):
        return sweep_slab(slab, norm_gains[0], project_in[0], project_out[0])

    def sweep_second(slab):
        return sweep_slab(slab, norm_gains[1], project_in[1], project_out[1])

    def sweep_third(slab):
        return sweep_slab(slab, norm_gains[2], project_in[2], project_out[2])

    def feed_forward(slab):
        normed = layer_norm(slab, norm_gains[3]).reshape(-1, WIDTH)
        hidden_units = jax.nn.gelu(jnp.dot(normed, expand_weight, preferred_element_type=jnp.float32)).astype(jnp.bfloat16)
        update = jnp.dot(hidden_units, reduce_weight, preferred_element_type=jnp.float32)
        return slab + update.reshape(slab.shape)
    state = jnp.transpose(state_field, (2, 1, 0, 3))
    state = jnp.transpose(lax.map(sweep_first, state), (2, 1, 0, 3))
    state = jnp.transpose(state, (2, 0, 1, 3))
    state = jnp.transpose(lax.map(sweep_second, state), (1, 2, 0, 3))
    state = lax.map(sweep_third, state)
    return lax.map(feed_forward, state)
```

```python
import functools

import jax
import jax.numpy as jnp
from jax import lax
from jax.experimental import pallas as pl
from jax.experimental.pallas import tpu as pltpu
from jax.sharding import PartitionSpec as P

HEADS = 8
HEAD_DIM = 32
LANES = 128
CHUNKS = 2
F32 = jnp.float32
BF16 = jnp.bfloat16
EXP_SCALE = HEAD_DIM ** (-0.5) * 1.4426950408889634


def norm_rows(rows, gain):
    center = rows - jnp.mean(rows, axis=-1, keepdims=True)
    spread = jnp.mean(center * center, axis=-1, keepdims=True)
    return (center * lax.rsqrt(spread + 1e-05) * gain).astype(BF16)


def head_masks(dtype):
    lane = lax.broadcasted_iota(jnp.int32, (1, LANES), 1)
    per = LANES // HEAD_DIM
    return [
        ((lane >= j * HEAD_DIM) & (lane < (j + 1) * HEAD_DIM)).astype(dtype)
        for j in range(per)
    ]


def pick_heads(parts):
    lane = lax.broadcasted_iota(jnp.int32, parts[0].shape, 1)
    out = parts[-1]
    for j in range(len(parts) - 2, -1, -1):
        out = jnp.where(lane < (j + 1) * HEAD_DIM, parts[j], out)
    return out


def softmax_keys(scores):
    peak = jnp.max(scores, axis=0, keepdims=True)
    expo = jnp.exp2((scores - peak) * EXP_SCALE)
    return expo * (1.0 / jnp.sum(expo, axis=0, keepdims=True))


def attend(query, key, value, masks):
    count, width = query.shape
    per = LANES // HEAD_DIM
    groups = width // LANES
    outs = []
    if count * per >= LANES:
        for g in range(groups):
            lanes = slice(g * LANES, (g + 1) * LANES)
            part = query[:, lanes]
            spread = jnp.concatenate([part * masks[j] for j in range(per)], axis=0)
            scores = lax.dot_general(
                key[:, lanes], spread, (((1,), (1,)), ((), ())), preferred_element_type=F32
            )
            weights = softmax_keys(scores).astype(BF16)
            mixed = lax.dot_general(
                weights, value[:, lanes], (((0,), (0,)), ((), ())), preferred_element_type=F32
            )
            outs.append(pick_heads([mixed[j * count : (j + 1) * count] for j in range(per)]))
    else:
        zero = jnp.zeros((count, LANES), query.dtype)
        rows = []
        for g in range(groups):
            part = query[:, g * LANES : (g + 1) * LANES]
            for j in range(per):
                rows.append(
                    jnp.concatenate(
                        [part * masks[j] if q == g else zero for q in range(groups)], axis=1
                    )
                )
        spread = jnp.concatenate(rows, axis=0)
        scores = lax.dot_general(
            key, spread, (((1,), (1,)), ((), ())), preferred_element_type=F32
        )
        weights = jnp.transpose(softmax_keys(scores)).astype(BF16)
        for g in range(groups):
            block = weights[g * per * count : (g + 1) * per * count]
            mixed = jnp.dot(
                block, value[:, g * LANES : (g + 1) * LANES], preferred_element_type=F32
            )
            outs.append(pick_heads([mixed[j * count : (j + 1) * count] for j in range(per)]))
    return jnp.concatenate(outs, axis=1).astype(BF16)


def best_block(total, want):
    block = min(total, want)
    while total % block:
        block -= 8
    return block


def project(source, weight_ref, sweep, lo, hi, write, block=512):
    total, read = source
    block = best_block(total, block)

    def step(i, carry):
        start = pl.multiple_of(i * block, block)
        out = jnp.dot(read(start, block), weight_ref[sweep, :, lo:hi], preferred_element_type=F32)
        write(start, block, out)
        return carry

    lax.fori_loop(0, total // block, step, 0)


def spread_lanes(ref, at, rows):
    for s in range(rows.shape[1] // LANES):
        ref[s, at, :] = rows[:, s * LANES : (s + 1) * LANES]


def strided(ref, start, count, stride):
    at = pl.ds(start, count, stride=stride)
    return jnp.concatenate([ref[s, at, :] for s in range(ref.shape[0])], axis=1)


def first_norm_kernel(dims, z0, zc, state_ref, gain_ref, out_ref, copy_ref, turn_ref):
    nx, ny, nz = dims
    gain = gain_ref[0:1, :]
    zlo, zhi = z0 // 8 * 8, -(-(z0 + zc) // 8) * 8
    zs = zhi - zlo
    width = gain.shape[1]

    def take(x, carry):
        rows = state_ref[pl.ds(x * ny, ny), zlo:zhi, :].reshape(ny * zs, width)
        spread_lanes(turn_ref, pl.ds(pl.multiple_of(x * ny * zs, 8), ny * zs), rows)
        return carry

    lax.fori_loop(0, nx, take, 0)

    def step(y, carry):
        for z in range(zc):
            rows = strided(turn_ref, y * zs + z0 - zlo + z, nx, ny * zs)
            at = pl.ds(pl.multiple_of((y * zc + z) * nx, nx), nx)
            copy_ref[at, :] = rows
            out_ref[at, :] = norm_rows(rows, gain)
        return carry

    lax.fori_loop(0, ny, step, 0)


def x_kernel(dims, zc, parts, groups, me_ref, *refs):
    nx, ny, nz = dims
    packs = refs[:parts]
    state_ref, gain_ref, win_ref, wout_ref = refs[parts : parts + 4]
    outs = refs[parts + 4 :]
    next_ref = outs[0]
    send = outs[1 : 1 + groups // 2]
    q_ref, k_ref, v_ref, mix_ref, turn_ref = outs[1 + groups // 2 :]
    width = gain_ref.shape[1]
    total = ny * zc * nx

    for d in range(parts):

        def write(start, block, out, d=d):
            at = pl.ds(start, block)
            if d == 0:
                q_ref[at, :] = out[:, :width].astype(BF16)
                out = out[:, width:]
            k_ref[d, at, :] = out[:, :width].astype(BF16)
            v_ref[d, at, :] = out[:, width:].astype(BF16)

        read = lambda start, block, d=d: packs[d][pl.ds(start, block), :]
        project((total, read), win_ref, 0, 0 if d == 0 else width, 3 * width, write)

    masks = head_masks(BF16)
    unroll = 4

    def pencil(i, carry):
        for u in range(unroll):
            at = pl.ds(pl.multiple_of((i * unroll + u) * nx, nx), nx)
            key = jnp.concatenate([k_ref[d, at, :] for d in range(parts)], axis=0)
            value = jnp.concatenate([v_ref[d, at, :] for d in range(parts)], axis=0)
            mix_ref[at, :] = attend(q_ref[at, :], key, value, masks)
        return carry

    lax.fori_loop(0, ny * zc // unroll, pencil, 0)

    block = best_block(total, 256)

    def residual(i, carry):
        at = pl.ds(pl.multiple_of(i * block, block), block)
        update = jnp.dot(mix_ref[at, :], wout_ref[0], preferred_element_type=F32)
        spread_lanes(turn_ref, at, state_ref[at, :] + update)
        return carry

    lax.fori_loop(0, total // block, residual, 0)

    me = me_ref[0]
    gain = gain_ref[1:2, :]
    per = nx // groups

    def turn(z, carry):
        for r in range(groups):
            for u in range(per):
                x = jnp.bitwise_xor(me, r) * per + u
                rows = strided(turn_ref, z * nx + x, ny, zc * nx)
                next_ref[z, x] = rows
                send[r // 2][r % 2, z, u] = norm_rows(rows, gain)
        return carry

    lax.fori_loop(0, zc, turn, 0)


def y_kernel(zc, per, ny, pieces, win_ref, *refs):
    half = pieces // 2
    near = refs[:half]
    far_ref = refs[half]
    outs = refs[half + 1 : 2 * half + 1]
    pack_ref = refs[2 * half + 1]
    width = win_ref.shape[1]
    total = zc * per * ny
    for j in range(pieces):

        def read(start, block, j=j):
            ref = near[j] if j < half else far_ref
            at = 0 if j < half else j - half
            return ref[at, pl.ds(start, block), :]

        def write(start, block, out, j=j):
            pack_ref[pl.ds(start // ny, block // ny), j] = out.reshape(block // ny, ny, 3 * width)

        project((total, read), win_ref, 1, 0, 3 * width, write)

    masks = head_masks(BF16)

    def pencil(i, carry):
        rows = pack_ref[i].reshape(pieces * ny, 3 * width).astype(BF16)
        mixed = attend(
            rows[:, :width], rows[:, width : 2 * width], rows[:, 2 * width :], masks
        )
        for j in range(pieces):
            outs[j % half][j // half, pl.ds(pl.multiple_of(i * ny, ny), ny), :] = mixed[
                j * ny : (j + 1) * ny
            ]
        return carry

    lax.fori_loop(0, zc * per, pencil, 0)


def y_merge_kernel(zc, per, ny, pieces, me_ref, state_ref, gain_ref, wout_ref, *refs):
    half = pieces // 2
    near = refs[:half]
    far_ref = refs[half]
    next_ref, send_ref = refs[half + 1 :]
    width = gain_ref.shape[1]
    me = me_ref[0]
    gain = gain_ref[2:3, :]
    for j in range(pieces):
        k, core = j % half, j // half
        mixed = near[k][0] if core == 0 else far_ref[k]
        update = jnp.dot(mixed, wout_ref[1], preferred_element_type=F32)
        update = update.reshape(zc, per, ny, width)
        x = jnp.bitwise_xor(me, 2 * k + core) * per
        rows = state_ref[:, pl.ds(x, per)] + update
        next_ref[:, pl.ds(x, per)] = rows
        send_ref[:, pl.ds(x, per)] = norm_rows(rows, gain)


def z_kernel(dims, zcs, parts, win_ref, wout_ref, gain_ref, expand_ref, reduce_ref, *refs):
    nx, ny, nz = dims
    chunks = len(zcs)
    states = refs[:chunks]
    packs = [refs[chunks * (1 + d) : chunks * (2 + d)] for d in range(parts)]
    out_ref = refs[chunks * (1 + parts)]
    q_ref, kv_ref, st_ref, mix_ref = refs[chunks * (1 + parts) + 1 :]
    width = gain_ref.shape[1]
    plane = nx * ny
    z0 = 0
    for c in range(chunks):
        base = z0 * plane
        for d in range(parts):

            def read(start, block, c=c, d=d):
                return packs[d][c][pl.ds(start, block), :]

            def write(start, block, out, d=d, base=base):
                at = pl.ds(pl.multiple_of(base + start, 8), block)
                if d == 0:
                    spread_lanes(q_ref, at, out[:, :width])
                    out = out[:, width:]
                spread_lanes(kv_ref.at[d], at, out)

            lo = 0 if d == 0 else width
            project((zcs[c] * plane, read), win_ref, 2, lo, 3 * width, write)
        z0 += zcs[c]

    masks = head_masks(BF16)
    unroll = 4

    def pencil(i, carry):
        for u in range(unroll):
            p = i * unroll + u
            query = strided(q_ref, p, nz, plane).astype(BF16)
            both = jnp.concatenate(
                [strided(kv_ref.at[d], p, nz, plane) for d in range(parts)], axis=0
            ).astype(BF16)
            key, value = both[:, :width], both[:, width:]
            mix_ref[pl.ds(pl.multiple_of(p * nz, nz), nz), :] = attend(query, key, value, masks)
        return carry

    lax.fori_loop(0, plane // unroll, pencil, 0)

    z0 = 0
    for c in range(chunks):
        spread_lanes(st_ref, pl.ds(z0 * plane, zcs[c] * plane), states[c][...])
        z0 += zcs[c]

    gain = gain_ref[3:4, :]
    group = best_block(plane, 16)

    def finish(i, carry):
        start = pl.multiple_of(i * group * nz, group * nz)
        at = pl.ds(start, group * nz)
        update = jnp.dot(mix_ref[at, :], wout_ref[2], preferred_element_type=F32)
        rows = jnp.concatenate(
            [strided(st_ref, i * group + u, nz, plane) for u in range(group)], axis=0
        )
        rows = rows + update
        normed = norm_rows(rows, gain)
        hidden = jax.nn.gelu(
            jnp.dot(normed, expand_ref[...], preferred_element_type=F32), approximate=True
        ).astype(BF16)
        out_ref[at, :] = rows + jnp.dot(hidden, reduce_ref[...], preferred_element_type=F32)
        return carry

    lax.fori_loop(0, plane // group, finish, 0)


VM = pl.BlockSpec(memory_space=pltpu.VMEM)
SM = pl.BlockSpec(memory_space=pltpu.SMEM)


def call(kernel, args, outs, scratch, flops, smem=()):
    single = not isinstance(outs, (list, tuple))
    shapes = [outs] if single else list(outs)
    got = pl.pallas_call(
        kernel,
        out_shape=shapes,
        in_specs=[SM if i in smem else VM for i in range(len(args))],
        out_specs=[VM] * len(shapes),
        scratch_shapes=scratch,
        compiler_params=pltpu.CompilerParams(vmem_limit_bytes=56 << 20),
        cost_estimate=pl.CostEstimate(flops=flops, bytes_accessed=1 << 20, transcendentals=0),
    )(*args)
    return got[0] if single else got


def shifted(array, axis, size, step):
    return lax.ppermute(array, axis, [(i, (i + step) % size) for i in range(size)])


def flipped(array, axis, size, mask):
    return lax.ppermute(array, axis, [(i, i ^ mask) for i in range(size)])


def on_device(sizes, state_field, norm_gains, project_in, project_out, expand_weight, reduce_weight):
    gx, gy, gz = sizes
    nx, ny, nz, width = state_field.shape
    dims = (nx, ny, nz)
    rows = nx * ny * nz
    half = max(gy // 2, 1)
    per = nx // gy
    shape = jax.ShapeDtypeStruct
    me = lax.axis_index("gy").astype(jnp.int32).reshape(1)
    state = state_field.reshape(nx * ny, nz, width)
    zc = nz // CHUNKS
    chunk_rows = nx * ny * zc
    cell = 2 * chunk_rows * width * width

    own, got = [], []
    for c in range(CHUNKS):
        span = -(-(c * zc + zc) // 8) * 8 - c * zc // 8 * 8
        normed, turned = call(
            functools.partial(first_norm_kernel, dims, c * zc, zc),
            (state, norm_gains),
            [shape((chunk_rows, width), BF16), shape((chunk_rows, width), F32)],
            [pltpu.VMEM((width // LANES, nx * ny * span, LANES), F32)],
            chunk_rows * width * 8,
        )
        own.append((normed, turned))
        got.append([shifted(normed, "gx", gx, d) for d in range(1, gx)])

    states, sends = [], []
    for c in range(CHUNKS):
        outs = call(
            functools.partial(x_kernel, dims, zc, gx, gy),
            (me, own[c][0], *got[c], own[c][1], norm_gains, project_in, project_out),
            [shape((zc, nx, ny, width), F32)]
            + [shape((2, zc, per, ny, width), BF16)] * half,
            [
                pltpu.VMEM((chunk_rows, width), BF16),
                pltpu.VMEM((gx, chunk_rows, width), BF16),
                pltpu.VMEM((gx, chunk_rows, width), BF16),
                pltpu.VMEM((chunk_rows, width), BF16),
                pltpu.VMEM((width // LANES, chunk_rows, LANES), F32),
            ],
            12 * cell,
            smem=(0,),
        )
        states.append(outs[0])
        sends.append(outs[1:])

    piece = zc * per * ny

    def exchange(blocks):
        near = [
            flipped(block, "gy", gy, 2 * k) if k else block for k, block in enumerate(blocks)
        ]
        far = flipped(jnp.stack([block[1] for block in near]), "gy", gy, 1)
        return near, far

    normeds = []
    for c in range(CHUNKS):
        near, far = exchange([s.reshape(2, piece, width) for s in sends[c]])
        mixed = call(
            functools.partial(y_kernel, zc, per, ny, 2 * half),
            (project_in, *near, far),
            [shape((2, piece, width), BF16)] * half,
            [pltpu.VMEM((zc * per, 2 * half, ny, 3 * width), F32)],
            12 * cell,
        )
        near, far = exchange(mixed)
        states[c], normed = call(
            functools.partial(y_merge_kernel, zc, per, ny, 2 * half),
            (me, states[c], norm_gains, project_out, *near, far),
            [shape((zc, nx, ny, width), F32), shape((zc, nx, ny, width), BF16)],
            [],
            2 * cell,
            smem=(0,),
        )
        normeds.append(normed.reshape(chunk_rows, width))

    theirs = [[shifted(n, "gz", gz, d) for n in normeds] for d in range(1, gz)]
    flat = [s.reshape(chunk_rows, width) for s in states]
    out = call(
        functools.partial(z_kernel, dims, [zc] * CHUNKS, gz),
        (
            project_in,
            project_out,
            norm_gains,
            expand_weight,
            reduce_weight,
            *flat,
            *normeds,
            *[t for per_shift in theirs for t in per_shift],
        ),
        shape((rows, width), F32),
        [
            pltpu.VMEM((width // LANES, rows, LANES), F32),
            pltpu.VMEM((gz, 2 * width // LANES, rows, LANES), F32),
            pltpu.VMEM((width // LANES, rows, LANES), F32),
            pltpu.VMEM((rows, width), BF16),
        ],
        20 * CHUNKS * cell,
    )
    return out.reshape(state_field.shape)


def solution(mesh):
    placed = (P("gx", "gy", "gz", None), P(), P(), P(), P(), P())
    sizes = tuple(mesh.shape[axis] for axis in ("gx", "gy", "gz"))
    return jax.shard_map(
        functools.partial(on_device, sizes),
        mesh=mesh,
        in_specs=placed,
        out_specs=P("gx", "gy", "gz", None),
        check_vma=False,
    )
```

```python
import functools

import jax
import jax.numpy as jnp
from jax import lax
from jax.experimental import pallas as pl
from jax.experimental.pallas import tpu as pltpu
from jax.sharding import PartitionSpec as P

HEADS = 8
HEAD_DIM = 32
LANES = 128
CHUNKS = 2
UNROLL = 16
Y_UNROLL = 4
F32 = jnp.float32
BF16 = jnp.bfloat16
EXP_SCALE = HEAD_DIM ** (-0.5) * 1.4426950408889634


def norm_rows(rows, gain):
    center = rows - jnp.mean(rows, axis=-1, keepdims=True)
    spread = jnp.mean(center * center, axis=-1, keepdims=True)
    return (center * lax.rsqrt(spread + 1e-05) * gain).astype(BF16)


def head_masks(dtype):
    lane = lax.broadcasted_iota(jnp.int32, (1, LANES), 1)
    per = LANES // HEAD_DIM
    return [
        ((lane >= j * HEAD_DIM) & (lane < (j + 1) * HEAD_DIM)).astype(dtype)
        for j in range(per)
    ]


def pick_heads(parts):
    lane = lax.broadcasted_iota(jnp.int32, parts[0].shape, 1)
    out = parts[-1]
    for j in range(len(parts) - 2, -1, -1):
        out = jnp.where(lane < (j + 1) * HEAD_DIM, parts[j], out)
    return out


def softmax_keys(scores, keys):
    cube = scores.reshape(scores.shape[0] // keys, keys, scores.shape[1])
    expo = jnp.exp2(cube - jnp.max(cube, axis=1, keepdims=True))
    weights = expo * (1.0 / jnp.sum(expo, axis=1, keepdims=True))
    return weights.reshape(scores.shape)


def attend(queries, keys, values, masks):
    count, width = queries[0].shape
    length = keys[0].shape[0]
    per = LANES // HEAD_DIM
    groups = width // LANES
    pack = max(1, LANES // length)
    joint = count * per < LANES
    batches = [range(i, min(i + pack, len(queries))) for i in range(0, len(queries), pack)]
    lanes = [slice(g * LANES, (g + 1) * LANES) for g in range(groups)]
    zero = jnp.zeros((count, LANES), BF16)

    def scores_of(p, g):
        blocks = [queries[p][:, lanes[g]] * masks[j] for j in range(per)]
        return jnp.concatenate(blocks, axis=0)

    def joint_scores(p):
        rows = []
        for g in range(groups):
            block = scores_of(p, g)
            fill = jnp.zeros_like(block)
            rows.append(jnp.concatenate([block if q == g else fill for q in range(groups)], axis=1))
        return jnp.concatenate(rows, axis=0)

    def dot_keys(key, spread):
        return lax.dot_general(key, spread, (((1,), (1,)), ((), ())), preferred_element_type=F32)

    if joint:
        raw = [[jnp.concatenate([dot_keys(keys[p], joint_scores(p)) for p in batch], axis=0)] for batch in batches]
    else:
        raw = [
            [
                jnp.concatenate([dot_keys(keys[p][:, lanes[g]], scores_of(p, g)) for p in batch], axis=0)
                for g in range(groups)
            ]
            for batch in batches
        ]
    weights = [[softmax_keys(part, length) for part in parts] for parts in raw]
    turned = [[jnp.transpose(part).astype(BF16) for part in parts] for parts in weights]
    mixed = []
    for batch, parts in zip(batches, turned):
        for g in range(groups):
            block = parts[0][g * per * count : (g + 1) * per * count] if joint else parts[g]
            fill = jnp.zeros((length, LANES), BF16)
            spread = jnp.concatenate(
                [
                    jnp.concatenate([values[p][:, lanes[g]] if p == q else fill for q in batch], axis=1)
                    for p in batch
                ],
                axis=0,
            )
            mixed.append(jnp.dot(block, spread, preferred_element_type=F32))
    outs = []
    for i, batch in enumerate(batches):
        for n in range(len(batch)):
            outs.append(
                jnp.concatenate(
                    [
                        pick_heads([mixed[i * groups + g][j * count : (j + 1) * count, lanes_of(n)] for j in range(per)])
                        for g in range(groups)
                    ],
                    axis=1,
                )
            )
    return outs


def lanes_of(n):
    return slice(n * LANES, (n + 1) * LANES)


def best_unroll(total, want):
    while total % want:
        want -= 1
    return want


def best_block(total, want):
    block = min(total, want)
    while total % block:
        block -= 8
    return block


def project(source, weight_ref, sweep, lo, hi, write, block=512):
    total, read = source
    block = best_block(total, block)

    def step(i, carry):
        start = pl.multiple_of(i * block, block)
        out = jnp.dot(read(start, block), weight_ref[sweep, :, lo:hi], preferred_element_type=F32)
        write(start, block, out)
        return carry

    lax.fori_loop(0, total // block, step, 0)


def spread_lanes(ref, at, rows):
    for s in range(rows.shape[1] // LANES):
        ref[s, at, :] = rows[:, s * LANES : (s + 1) * LANES]


def strided(ref, start, count, stride):
    at = pl.ds(start, count, stride=stride)
    return jnp.concatenate([ref[s, at, :] for s in range(ref.shape[0])], axis=1)


def first_norm_kernel(dims, z0, zc, state_ref, gain_ref, out_ref, copy_ref, turn_ref):
    nx, ny, nz = dims
    gain = gain_ref[0:1, :]
    zlo, zhi = z0 // 8 * 8, -(-(z0 + zc) // 8) * 8
    zs = zhi - zlo
    width = gain.shape[1]

    def take(x, carry):
        rows = state_ref[pl.ds(x * ny, ny), zlo:zhi, :].reshape(ny * zs, width)
        spread_lanes(turn_ref, pl.ds(pl.multiple_of(x * ny * zs, 8), ny * zs), rows)
        return carry

    lax.fori_loop(0, nx, take, 0)

    def step(y, carry):
        for z in range(zc):
            rows = strided(turn_ref, y * zs + z0 - zlo + z, nx, ny * zs)
            at = pl.ds(pl.multiple_of((y * zc + z) * nx, nx), nx)
            copy_ref[at, :] = rows
            out_ref[at, :] = norm_rows(rows, gain)
        return carry

    lax.fori_loop(0, ny, step, 0)


def x_kernel(dims, zc, parts, groups, me_ref, *refs):
    nx, ny, nz = dims
    packs = refs[:parts]
    state_ref, gain_ref, win_ref, wout_ref = refs[parts : parts + 4]
    outs = refs[parts + 4 :]
    next_ref = outs[0]
    send = outs[1 : 1 + groups // 2]
    q_ref, k_ref, v_ref, mix_ref, turn_ref = outs[1 + groups // 2 :]
    width = gain_ref.shape[1]
    total = ny * zc * nx

    for d in range(parts):

        def write(start, block, out, d=d):
            at = pl.ds(start, block)
            if d == 0:
                q_ref[at, :] = out[:, :width] * EXP_SCALE
                out = out[:, width:]
            k_ref[d, at, :] = out[:, :width].astype(BF16)
            v_ref[d, at, :] = out[:, width:].astype(BF16)

        read = lambda start, block, d=d: packs[d][pl.ds(start, block), :]
        project((total, read), win_ref, 0, 0 if d == 0 else width, 3 * width, write)

    masks = head_masks(BF16)
    unroll = best_unroll(ny * zc, UNROLL)

    def pencil(i, carry):
        ats = [pl.ds(pl.multiple_of((i * unroll + u) * nx, nx), nx) for u in range(unroll)]
        queries = [q_ref[at, :].astype(BF16) for at in ats]
        keys = [jnp.concatenate([k_ref[d, at, :] for d in range(parts)], axis=0) for at in ats]
        values = [jnp.concatenate([v_ref[d, at, :] for d in range(parts)], axis=0) for at in ats]
        for at, mixed in zip(ats, attend(queries, keys, values, masks)):
            mix_ref[at, :] = mixed.astype(BF16)
        return carry

    lax.fori_loop(0, ny * zc // unroll, pencil, 0)

    block = best_block(total, 256)

    def residual(i, carry):
        at = pl.ds(pl.multiple_of(i * block, block), block)
        update = jnp.dot(mix_ref[at, :], wout_ref[0], preferred_element_type=F32)
        spread_lanes(turn_ref, at, state_ref[at, :] + update)
        return carry

    lax.fori_loop(0, total // block, residual, 0)

    me = me_ref[0]
    gain = gain_ref[1:2, :]
    per = nx // groups

    def turn(z, carry):
        for r in range(groups):
            for u in range(per):
                x = jnp.bitwise_xor(me, r) * per + u
                rows = strided(turn_ref, z * nx + x, ny, zc * nx)
                next_ref[z, x] = rows
                send[r // 2][r % 2, z, u] = norm_rows(rows, gain)
        return carry

    lax.fori_loop(0, zc, turn, 0)


def y_kernel(zc, per, ny, pieces, win_ref, *refs):
    half = pieces // 2
    near = refs[:half]
    far_ref = refs[half]
    outs = refs[half + 1 : 2 * half + 1]
    pack_ref = refs[2 * half + 1]
    width = win_ref.shape[1]
    total = zc * per * ny
    for j in range(pieces):

        def read(start, block, j=j):
            ref = near[j] if j < half else far_ref
            at = 0 if j < half else j - half
            return ref[at, pl.ds(start, block), :]

        def write(start, block, out, j=j):
            pack_ref[pl.ds(start // ny, block // ny), j] = out.reshape(block // ny, ny, 3 * width)

        project((total, read), win_ref, 1, 0, 3 * width, write)

    masks = head_masks(BF16)

    unroll = best_unroll(zc * per, Y_UNROLL)

    def pencil(i, carry):
        rows = [
            pack_ref[i * unroll + u].reshape(pieces * ny, 3 * width) for u in range(unroll)
        ]
        queries = [(r[:, :width] * EXP_SCALE).astype(BF16) for r in rows]
        keys = [r[:, width : 2 * width].astype(BF16) for r in rows]
        values = [r[:, 2 * width :].astype(BF16) for r in rows]
        for u, mixed in enumerate(attend(queries, keys, values, masks)):
            at = pl.ds(pl.multiple_of((i * unroll + u) * ny, ny), ny)
            for j in range(pieces):
                outs[j % half][j // half, at, :] = mixed[j * ny : (j + 1) * ny].astype(BF16)
        return carry

    lax.fori_loop(0, zc * per // unroll, pencil, 0)


def y_merge_kernel(zc, per, ny, pieces, me_ref, state_ref, gain_ref, wout_ref, *refs):
    half = pieces // 2
    near = refs[:half]
    far_ref = refs[half]
    next_ref, send_ref = refs[half + 1 :]
    width = gain_ref.shape[1]
    me = me_ref[0]
    gain = gain_ref[2:3, :]
    for j in range(pieces):
        k, core = j % half, j // half
        mixed = near[k][0] if core == 0 else far_ref[k]
        update = jnp.dot(mixed, wout_ref[1], preferred_element_type=F32)
        update = update.reshape(zc, per, ny, width)
        x = jnp.bitwise_xor(me, 2 * k + core) * per
        rows = state_ref[:, pl.ds(x, per)] + update
        next_ref[:, pl.ds(x, per)] = rows
        send_ref[:, pl.ds(x, per)] = norm_rows(rows, gain)


def z_kernel(dims, zcs, parts, win_ref, wout_ref, gain_ref, expand_ref, reduce_ref, *refs):
    nx, ny, nz = dims
    chunks = len(zcs)
    states = refs[:chunks]
    packs = [refs[chunks * (1 + d) : chunks * (2 + d)] for d in range(parts)]
    out_ref = refs[chunks * (1 + parts)]
    q_ref, kv_ref, st_ref, mix_ref = refs[chunks * (1 + parts) + 1 :]
    width = gain_ref.shape[1]
    plane = nx * ny
    z0 = 0
    for c in range(chunks):
        base = z0 * plane
        for d in range(parts):

            def read(start, block, c=c, d=d):
                return packs[d][c][pl.ds(start, block), :]

            def write(start, block, out, d=d, base=base):
                at = pl.ds(pl.multiple_of(base + start, 8), block)
                if d == 0:
                    spread_lanes(q_ref, at, out[:, :width] * EXP_SCALE)
                    out = out[:, width:]
                spread_lanes(kv_ref.at[d], at, out)

            lo = 0 if d == 0 else width
            project((zcs[c] * plane, read), win_ref, 2, lo, 3 * width, write)
        z0 += zcs[c]

    masks = head_masks(BF16)
    unroll = best_unroll(plane, UNROLL)

    def pencil(i, carry):
        ps = [i * unroll + u for u in range(unroll)]
        queries = [strided(q_ref, p, nz, plane).astype(BF16) for p in ps]
        both = [
            jnp.concatenate([strided(kv_ref.at[d], p, nz, plane) for d in range(parts)], axis=0).astype(BF16)
            for p in ps
        ]
        keys = [b[:, :width] for b in both]
        values = [b[:, width:] for b in both]
        for p, mixed in zip(ps, attend(queries, keys, values, masks)):
            mix_ref[pl.ds(pl.multiple_of(p * nz, nz), nz), :] = mixed.astype(BF16)
        return carry

    lax.fori_loop(0, plane // unroll, pencil, 0)

    z0 = 0
    for c in range(chunks):
        spread_lanes(st_ref, pl.ds(z0 * plane, zcs[c] * plane), states[c][...])
        z0 += zcs[c]

    gain = gain_ref[3:4, :]
    group = best_block(plane, 16)

    def finish(i, carry):
        start = pl.multiple_of(i * group * nz, group * nz)
        at = pl.ds(start, group * nz)
        update = jnp.dot(mix_ref[at, :], wout_ref[2], preferred_element_type=F32)
        rows = jnp.concatenate(
            [strided(st_ref, i * group + u, nz, plane) for u in range(group)], axis=0
        )
        rows = rows + update
        normed = norm_rows(rows, gain)
        hidden = jax.nn.gelu(
            jnp.dot(normed, expand_ref[...], preferred_element_type=F32), approximate=True
        ).astype(BF16)
        out_ref[at, :] = rows + jnp.dot(hidden, reduce_ref[...], preferred_element_type=F32)
        return carry

    lax.fori_loop(0, plane // group, finish, 0)


VM = pl.BlockSpec(memory_space=pltpu.VMEM)
SM = pl.BlockSpec(memory_space=pltpu.SMEM)


def call(kernel, args, outs, scratch, flops, smem=()):
    single = not isinstance(outs, (list, tuple))
    shapes = [outs] if single else list(outs)
    got = pl.pallas_call(
        kernel,
        out_shape=shapes,
        in_specs=[SM if i in smem else VM for i in range(len(args))],
        out_specs=[VM] * len(shapes),
        scratch_shapes=scratch,
        compiler_params=pltpu.CompilerParams(vmem_limit_bytes=56 << 20),
        cost_estimate=pl.CostEstimate(flops=flops, bytes_accessed=1 << 20, transcendentals=0),
    )(*args)
    return got[0] if single else got


def shifted(array, axis, size, step):
    return lax.ppermute(array, axis, [(i, (i + step) % size) for i in range(size)])


def flipped(array, axis, size, mask):
    return lax.ppermute(array, axis, [(i, i ^ mask) for i in range(size)])


def on_device(sizes, state_field, norm_gains, project_in, project_out, expand_weight, reduce_weight):
    gx, gy, gz = sizes
    nx, ny, nz, width = state_field.shape
    dims = (nx, ny, nz)
    rows = nx * ny * nz
    half = max(gy // 2, 1)
    per = nx // gy
    shape = jax.ShapeDtypeStruct
    me = lax.axis_index("gy").astype(jnp.int32).reshape(1)
    state = state_field.reshape(nx * ny, nz, width)
    zc = nz // CHUNKS
    chunk_rows = nx * ny * zc
    cell = 2 * chunk_rows * width * width

    own, got = [], []
    for c in range(CHUNKS):
        span = -(-(c * zc + zc) // 8) * 8 - c * zc // 8 * 8
        normed, turned = call(
            functools.partial(first_norm_kernel, dims, c * zc, zc),
            (state, norm_gains),
            [shape((chunk_rows, width), BF16), shape((chunk_rows, width), F32)],
            [pltpu.VMEM((width // LANES, nx * ny * span, LANES), F32)],
            chunk_rows * width * 8,
        )
        own.append((normed, turned))
        got.append([shifted(normed, "gx", gx, d) for d in range(1, gx)])

    states, sends = [], []
    for c in range(CHUNKS):
        outs = call(
            functools.partial(x_kernel, dims, zc, gx, gy),
            (me, own[c][0], *got[c], own[c][1], norm_gains, project_in, project_out),
            [shape((zc, nx, ny, width), F32)]
            + [shape((2, zc, per, ny, width), BF16)] * half,
            [
                pltpu.VMEM((chunk_rows, width), F32),
                pltpu.VMEM((gx, chunk_rows, width), BF16),
                pltpu.VMEM((gx, chunk_rows, width), BF16),
                pltpu.VMEM((chunk_rows, width), BF16),
                pltpu.VMEM((width // LANES, chunk_rows, LANES), F32),
            ],
            12 * cell,
            smem=(0,),
        )
        states.append(outs[0])
        sends.append(outs[1:])

    piece = zc * per * ny

    def exchange(blocks):
        near = [
            flipped(block, "gy", gy, 2 * k) if k else block for k, block in enumerate(blocks)
        ]
        far = flipped(jnp.stack([block[1] for block in near]), "gy", gy, 1)
        return near, far

    normeds = []
    for c in range(CHUNKS):
        near, far = exchange([s.reshape(2, piece, width) for s in sends[c]])
        mixed = call(
            functools.partial(y_kernel, zc, per, ny, 2 * half),
            (project_in, *near, far),
            [shape((2, piece, width), BF16)] * half,
            [pltpu.VMEM((zc * per, 2 * half, ny, 3 * width), F32)],
            12 * cell,
        )
        near, far = exchange(mixed)
        states[c], normed = call(
            functools.partial(y_merge_kernel, zc, per, ny, 2 * half),
            (me, states[c], norm_gains, project_out, *near, far),
            [shape((zc, nx, ny, width), F32), shape((zc, nx, ny, width), BF16)],
            [],
            2 * cell,
            smem=(0,),
        )
        normeds.append(normed.reshape(chunk_rows, width))

    theirs = [[shifted(n, "gz", gz, d) for n in normeds] for d in range(1, gz)]
    flat = [s.reshape(chunk_rows, width) for s in states]
    out = call(
        functools.partial(z_kernel, dims, [zc] * CHUNKS, gz),
        (
            project_in,
            project_out,
            norm_gains,
            expand_weight,
            reduce_weight,
            *flat,
            *normeds,
            *[t for per_shift in theirs for t in per_shift],
        ),
        shape((rows, width), F32),
        [
            pltpu.VMEM((width // LANES, rows, LANES), F32),
            pltpu.VMEM((gz, 2 * width // LANES, rows, LANES), F32),
            pltpu.VMEM((width // LANES, rows, LANES), F32),
            pltpu.VMEM((rows, width), BF16),
        ],
        20 * CHUNKS * cell,
    )
    return out.reshape(state_field.shape)


def solution(mesh):
    placed = (P("gx", "gy", "gz", None), P(), P(), P(), P(), P())
    sizes = tuple(mesh.shape[axis] for axis in ("gx", "gy", "gz"))
    return jax.shard_map(
        functools.partial(on_device, sizes),
        mesh=mesh,
        in_specs=placed,
        out_specs=P("gx", "gy", "gz", None),
        check_vma=False,
    )
```

```python
import functools

import jax
import jax.numpy as jnp
from jax import lax
from jax.experimental import pallas as pl
from jax.experimental.pallas import tpu as pltpu
from jax.sharding import PartitionSpec as P

HEAD_DIM = 32
LANES = 128
CHUNKS = 2
UNROLL = 32
GROUP = 32
Y_UNROLL = 8
F32 = jnp.float32
BF16 = jnp.bfloat16
EXP_SCALE = HEAD_DIM ** (-0.5) * 1.4426950408889634


def norm_rows(rows, gain):
    center = rows - jnp.mean(rows, axis=-1, keepdims=True)
    spread = jnp.mean(center * center, axis=-1, keepdims=True)
    return (center * lax.rsqrt(spread + 1e-05) * gain).astype(BF16)


def gelu(v):
    half = 0.5 * v
    return half * jnp.tanh(v * (0.7978845608028654 + 0.035677408136300125 * (v * v))) + half


def head_masks(dtype):
    lane = lax.broadcasted_iota(jnp.int32, (1, LANES), 1)
    per = LANES // HEAD_DIM
    return [
        ((lane >= j * HEAD_DIM) & (lane < (j + 1) * HEAD_DIM)).astype(dtype)
        for j in range(per)
    ]


def pick_heads(parts):
    lane = lax.broadcasted_iota(jnp.int32, parts[0].shape, 1)
    out = parts[-1]
    for j in range(len(parts) - 2, -1, -1):
        out = jnp.where(lane < (j + 1) * HEAD_DIM, parts[j], out)
    return out


def softmax_keys(scores, keys):
    cube = scores.reshape(scores.shape[0] // keys, keys, scores.shape[1])
    expo = jnp.exp2(cube - jnp.max(cube, axis=1, keepdims=True))
    weights = expo * (1.0 / jnp.sum(expo, axis=1, keepdims=True))
    return weights.reshape(scores.shape)


def attend(queries, keys, values, masks):
    count, width = queries[0].shape
    length = keys[0].shape[0]
    per = LANES // HEAD_DIM
    groups = width // LANES
    pack = max(1, LANES // length)
    joint = count * per < LANES
    batches = [range(i, min(i + pack, len(queries))) for i in range(0, len(queries), pack)]
    lanes = [slice(g * LANES, (g + 1) * LANES) for g in range(groups)]
    zero = jnp.zeros((count, LANES), BF16)

    def scores_of(p, g):
        blocks = [queries[p][:, lanes[g]] * masks[j] for j in range(per)]
        return jnp.concatenate(blocks, axis=0)

    def joint_scores(p):
        rows = []
        for g in range(groups):
            block = scores_of(p, g)
            fill = jnp.zeros_like(block)
            rows.append(jnp.concatenate([block if q == g else fill for q in range(groups)], axis=1))
        return jnp.concatenate(rows, axis=0)

    def dot_keys(key, spread):
        return lax.dot_general(key, spread, (((1,), (1,)), ((), ())), preferred_element_type=F32)

    if joint:
        raw = [[jnp.concatenate([dot_keys(keys[p], joint_scores(p)) for p in batch], axis=0)] for batch in batches]
    else:
        raw = [
            [
                jnp.concatenate([dot_keys(keys[p][:, lanes[g]], scores_of(p, g)) for p in batch], axis=0)
                for g in range(groups)
            ]
            for batch in batches
        ]
    weights = [[softmax_keys(part, length) for part in parts] for parts in raw]
    turned = [[jnp.transpose(part).astype(BF16) for part in parts] for parts in weights]
    mixed = []
    for batch, parts in zip(batches, turned):
        for g in range(groups):
            block = parts[0][g * per * count : (g + 1) * per * count] if joint else parts[g]
            fill = jnp.zeros((length, LANES), BF16)
            spread = jnp.concatenate(
                [
                    jnp.concatenate([values[p][:, lanes[g]] if p == q else fill for q in batch], axis=1)
                    for p in batch
                ],
                axis=0,
            )
            mixed.append(jnp.dot(block, spread, preferred_element_type=F32))
    outs = []
    for i, batch in enumerate(batches):
        for n in range(len(batch)):
            outs.append(
                jnp.concatenate(
                    [
                        pick_heads([mixed[i * groups + g][j * count : (j + 1) * count, lanes_of(n)] for j in range(per)])
                        for g in range(groups)
                    ],
                    axis=1,
                )
            )
    return outs


def lanes_of(n):
    return slice(n * LANES, (n + 1) * LANES)


def best_unroll(total, want):
    while total % want:
        want -= 1
    return want


def best_block(total, want):
    block = min(total, want)
    while total % block:
        block -= 8
    return block


def project(source, weight_ref, sweep, lo, hi, write, block=512):
    total, read = source
    block = best_block(total, block)

    def step(i, carry):
        start = pl.multiple_of(i * block, block)
        out = jnp.dot(read(start, block), weight_ref[sweep, :, lo:hi], preferred_element_type=F32)
        write(start, block, out)
        return carry

    lax.fori_loop(0, total // block, step, 0)


def spread_lanes(ref, at, rows):
    for s in range(rows.shape[1] // LANES):
        ref[s, at, :] = rows[:, s * LANES : (s + 1) * LANES]


def strided(ref, start, count, stride):
    at = pl.ds(start, count, stride=stride)
    return jnp.concatenate([ref[s, at, :] for s in range(ref.shape[0])], axis=1)


def first_norm_kernel(dims, z0, zc, state_ref, gain_ref, out_ref, copy_ref, turn_ref):
    nx, ny, _ = dims
    gain = gain_ref[0:1, :]
    zlo, zhi = z0 // 8 * 8, -(-(z0 + zc) // 8) * 8
    zs = zhi - zlo
    width = gain.shape[1]

    def take(x, carry):
        rows = state_ref[pl.ds(x * ny, ny), zlo:zhi, :].reshape(ny * zs, width)
        spread_lanes(turn_ref, pl.ds(pl.multiple_of(x * ny * zs, 8), ny * zs), rows)
        return carry

    lax.fori_loop(0, nx, take, 0)

    def step(y, carry):
        rows = jnp.concatenate(
            [strided(turn_ref, y * zs + z0 - zlo + z, nx, ny * zs) for z in range(zc)], axis=0
        )
        at = pl.ds(pl.multiple_of(y * zc * nx, zc * nx), zc * nx)
        copy_ref[at, :] = rows
        out_ref[at, :] = norm_rows(rows, gain)
        return carry

    lax.fori_loop(0, ny, step, 0)


def x_kernel(dims, zc, parts, groups, me_ref, *refs):
    nx, ny, _ = dims
    packs = refs[:parts]
    state_ref, gain_ref, win_ref, wout_ref = refs[parts : parts + 4]
    outs = refs[parts + 4 :]
    next_ref = outs[0]
    send = outs[1 : 1 + groups // 2]
    q_ref, k_ref, v_ref, mix_ref, turn_ref = outs[1 + groups // 2 :]
    width = gain_ref.shape[1]
    total = ny * zc * nx

    for d in range(parts):

        def write(start, block, out, d=d):
            at = pl.ds(start, block)
            if d == 0:
                q_ref[at, :] = out[:, :width] * EXP_SCALE
                out = out[:, width:]
            k_ref[d, at, :] = out[:, :width].astype(BF16)
            v_ref[d, at, :] = out[:, width:].astype(BF16)

        read = lambda start, block, d=d: packs[d][pl.ds(start, block), :]
        project((total, read), win_ref, 0, 0 if d == 0 else width, 3 * width, write)

    masks = head_masks(BF16)
    unroll = best_unroll(ny * zc, UNROLL)

    def pencil(i, carry):
        ats = [pl.ds(pl.multiple_of((i * unroll + u) * nx, nx), nx) for u in range(unroll)]
        queries = [q_ref[at, :].astype(BF16) for at in ats]
        keys = [jnp.concatenate([k_ref[d, at, :] for d in range(parts)], axis=0) for at in ats]
        values = [jnp.concatenate([v_ref[d, at, :] for d in range(parts)], axis=0) for at in ats]
        for at, mixed in zip(ats, attend(queries, keys, values, masks)):
            mix_ref[at, :] = mixed.astype(BF16)
        return carry

    lax.fori_loop(0, ny * zc // unroll, pencil, 0)

    block = best_block(total, 256)

    def residual(i, carry):
        at = pl.ds(pl.multiple_of(i * block, block), block)
        update = jnp.dot(mix_ref[at, :], wout_ref[0], preferred_element_type=F32)
        spread_lanes(turn_ref, at, state_ref[at, :] + update)
        return carry

    lax.fori_loop(0, total // block, residual, 0)

    me = me_ref[0]
    gain = gain_ref[1:2, :]
    per = nx // groups

    def turn(z, carry):
        spots = [(r, u) for r in range(groups) for u in range(per)]
        xs = [jnp.bitwise_xor(me, r) * per + u for r, u in spots]
        rows = jnp.concatenate([strided(turn_ref, z * nx + x, ny, zc * nx) for x in xs], axis=0)
        normed = norm_rows(rows, gain)
        for i, ((r, u), x) in enumerate(zip(spots, xs)):
            next_ref[z, x] = rows[i * ny : (i + 1) * ny]
            send[r // 2][r % 2, z, u] = normed[i * ny : (i + 1) * ny]
        return carry

    lax.fori_loop(0, zc, turn, 0)


def y_kernel(zc, per, ny, pieces, win_ref, *refs):
    half = pieces // 2
    near = refs[:half]
    far_ref = refs[half]
    outs = refs[half + 1 : 2 * half + 1]
    pack_ref = refs[2 * half + 1]
    width = win_ref.shape[1]
    total = zc * per * ny
    for j in range(pieces):

        def read(start, block, j=j):
            ref = near[j] if j < half else far_ref
            at = 0 if j < half else j - half
            return ref[at, pl.ds(start, block), :]

        def write(start, block, out, j=j):
            pack_ref[pl.ds(start // ny, block // ny), j] = out.reshape(block // ny, ny, 3 * width)

        project((total, read), win_ref, 1, 0, 3 * width, write)

    masks = head_masks(BF16)

    unroll = best_unroll(zc * per, Y_UNROLL)

    def pencil(i, carry):
        rows = [
            pack_ref[i * unroll + u].reshape(pieces * ny, 3 * width) for u in range(unroll)
        ]
        queries = [(r[:, :width] * EXP_SCALE).astype(BF16) for r in rows]
        keys = [r[:, width : 2 * width].astype(BF16) for r in rows]
        values = [r[:, 2 * width :].astype(BF16) for r in rows]
        for u, mixed in enumerate(attend(queries, keys, values, masks)):
            at = pl.ds(pl.multiple_of((i * unroll + u) * ny, ny), ny)
            for j in range(pieces):
                outs[j % half][j // half, at, :] = mixed[j * ny : (j + 1) * ny].astype(BF16)
        return carry

    lax.fori_loop(0, zc * per // unroll, pencil, 0)


def y_merge_kernel(zc, per, ny, pieces, me_ref, state_ref, gain_ref, wout_ref, *refs):
    half = pieces // 2
    near = refs[:half]
    far_ref = refs[half]
    next_ref, send_ref = refs[half + 1 :]
    width = gain_ref.shape[1]
    me = me_ref[0]
    gain = gain_ref[2:3, :]
    for j in range(pieces):
        k, core = j % half, j // half
        mixed = near[k][0] if core == 0 else far_ref[k]
        update = jnp.dot(mixed, wout_ref[1], preferred_element_type=F32)
        update = update.reshape(zc, per, ny, width)
        x = jnp.bitwise_xor(me, 2 * k + core) * per
        rows = state_ref[:, pl.ds(x, per)] + update
        next_ref[:, pl.ds(x, per)] = rows
        send_ref[:, pl.ds(x, per)] = norm_rows(rows, gain)


def z_kernel(dims, zcs, parts, win_ref, wout_ref, gain_ref, expand_ref, reduce_ref, *refs):
    nx, ny, nz = dims
    chunks = len(zcs)
    states = refs[:chunks]
    packs = [refs[chunks * (1 + d) : chunks * (2 + d)] for d in range(parts)]
    out_ref = refs[chunks * (1 + parts)]
    q_ref, kv_ref, st_ref, mix_ref = refs[chunks * (1 + parts) + 1 :]
    width = gain_ref.shape[1]
    plane = nx * ny
    z0 = 0
    for c in range(chunks):
        base = z0 * plane
        for d in range(parts):

            def read(start, block, c=c, d=d):
                return packs[d][c][pl.ds(start, block), :]

            def write(start, block, out, d=d, base=base):
                at = pl.ds(pl.multiple_of(base + start, 8), block)
                if d == 0:
                    spread_lanes(q_ref, at, out[:, :width] * EXP_SCALE)
                    out = out[:, width:]
                spread_lanes(kv_ref.at[d], at, out)

            lo = 0 if d == 0 else width
            project((zcs[c] * plane, read), win_ref, 2, lo, 3 * width, write)
        z0 += zcs[c]

    masks = head_masks(BF16)
    unroll = best_unroll(plane, UNROLL)

    def pencil(i, carry):
        ps = [i * unroll + u for u in range(unroll)]
        queries = [strided(q_ref, p, nz, plane).astype(BF16) for p in ps]
        both = [
            jnp.concatenate([strided(kv_ref.at[d], p, nz, plane) for d in range(parts)], axis=0).astype(BF16)
            for p in ps
        ]
        keys = [b[:, :width] for b in both]
        values = [b[:, width:] for b in both]
        for p, mixed in zip(ps, attend(queries, keys, values, masks)):
            mix_ref[pl.ds(pl.multiple_of(p * nz, nz), nz), :] = mixed.astype(BF16)
        return carry

    lax.fori_loop(0, plane // unroll, pencil, 0)

    z0 = 0
    for c in range(chunks):
        spread_lanes(st_ref, pl.ds(z0 * plane, zcs[c] * plane), states[c][...])
        z0 += zcs[c]

    gain = gain_ref[3:4, :]
    group = best_block(plane, GROUP)

    def finish(i, carry):
        start = pl.multiple_of(i * group * nz, group * nz)
        at = pl.ds(start, group * nz)
        update = jnp.dot(mix_ref[at, :], wout_ref[2], preferred_element_type=F32)
        rows = jnp.concatenate(
            [strided(st_ref, i * group + u, nz, plane) for u in range(group)], axis=0
        )
        rows = rows + update
        normed = norm_rows(rows, gain)
        hidden = gelu(jnp.dot(normed, expand_ref[...], preferred_element_type=F32)).astype(BF16)
        out_ref[at, :] = rows + jnp.dot(hidden, reduce_ref[...], preferred_element_type=F32)
        return carry

    lax.fori_loop(0, plane // group, finish, 0)


VM = pl.BlockSpec(memory_space=pltpu.VMEM)
SM = pl.BlockSpec(memory_space=pltpu.SMEM)


def call(kernel, args, outs, scratch, flops, smem=()):
    return call_inner(kernel, args, outs, scratch, flops, smem)


def call_inner(kernel, args, outs, scratch, flops, smem):
    space = sum(a.size * a.dtype.itemsize for a in args) + (4 << 20)
    single = not isinstance(outs, (list, tuple))
    shapes = [outs] if single else list(outs)
    space += sum(a.size * a.dtype.itemsize for a in shapes)
    space += sum(a.size * jnp.dtype(a.dtype).itemsize for a in (jax.ShapeDtypeStruct(m.shape, m.dtype) for m in scratch))
    got = pl.pallas_call(
        kernel,
        out_shape=shapes,
        in_specs=[SM if i in smem else VM for i in range(len(args))],
        out_specs=[VM] * len(shapes),
        scratch_shapes=scratch,
        compiler_params=pltpu.CompilerParams(vmem_limit_bytes=min(space, 60 << 20)),
        cost_estimate=pl.CostEstimate(flops=flops, bytes_accessed=1 << 20, transcendentals=0),
    )(*args)
    return got[0] if single else got


def shifted(array, axis, size, step):
    return lax.ppermute(array, axis, [(i, (i + step) % size) for i in range(size)])


def flipped(array, axis, size, mask):
    return lax.ppermute(array, axis, [(i, i ^ mask) for i in range(size)])


def on_device(sizes, state_field, norm_gains, project_in, project_out, expand_weight, reduce_weight):
    gx, gy, gz = sizes
    nx, ny, nz, width = state_field.shape
    dims = (nx, ny, nz)
    rows = nx * ny * nz
    half = max(gy // 2, 1)
    per = nx // gy
    shape = jax.ShapeDtypeStruct
    me = lax.axis_index("gy").astype(jnp.int32).reshape(1)
    state = state_field.reshape(nx * ny, nz, width)
    zc = nz // CHUNKS
    chunk_rows = nx * ny * zc
    cell = 2 * chunk_rows * width * width

    own, got = [], []
    for c in range(CHUNKS):
        span = -(-(c * zc + zc) // 8) * 8 - c * zc // 8 * 8
        normed, turned = call(
            functools.partial(first_norm_kernel, dims, c * zc, zc),
            (state, norm_gains),
            [shape((chunk_rows, width), BF16), shape((chunk_rows, width), F32)],
            [pltpu.VMEM((width // LANES, nx * ny * span, LANES), F32)],
            chunk_rows * width * 8,
        )
        own.append((normed, turned))
        got.append([shifted(normed, "gx", gx, d) for d in range(1, gx)])

    states, sends = [], []
    for c in range(CHUNKS):
        outs = call(
            functools.partial(x_kernel, dims, zc, gx, gy),
            (me, own[c][0], *got[c], own[c][1], norm_gains, project_in, project_out),
            [shape((zc, nx, ny, width), F32)]
            + [shape((2, zc, per, ny, width), BF16)] * half,
            [
                pltpu.VMEM((chunk_rows, width), F32),
                pltpu.VMEM((gx, chunk_rows, width), BF16),
                pltpu.VMEM((gx, chunk_rows, width), BF16),
                pltpu.VMEM((chunk_rows, width), BF16),
                pltpu.VMEM((width // LANES, chunk_rows, LANES), F32),
            ],
            12 * cell,
            smem=(0,),
        )
        states.append(outs[0])
        sends.append(outs[1:])

    piece = zc * per * ny

    def exchange(blocks):
        near = [
            flipped(block, "gy", gy, 2 * k) if k else block for k, block in enumerate(blocks)
        ]
        second = jnp.stack([block[1] for block in near])
        far = flipped(second, "gy", gy, 1)
        return near, far

    normeds = []
    for c in range(CHUNKS):
        near, far = exchange([s.reshape(2, piece, width) for s in sends[c]])
        mixed = call(
            functools.partial(y_kernel, zc, per, ny, 2 * half),
            (project_in, *near, far),
            [shape((2, piece, width), BF16)] * half,
            [pltpu.VMEM((zc * per, 2 * half, ny, 3 * width), F32)],
            12 * cell,
        )
        near, far = exchange(mixed)
        states[c], normed = call(
            functools.partial(y_merge_kernel, zc, per, ny, 2 * half),
            (me, states[c], norm_gains, project_out, *near, far),
            [shape((zc, nx, ny, width), F32), shape((zc, nx, ny, width), BF16)],
            [],
            2 * cell,
            smem=(0,),
        )
        normeds.append(normed.reshape(chunk_rows, width))

    theirs = []
    for d in range(1, gz):
        theirs.append([])
        for normed in normeds:
            theirs[-1].append(shifted(normed, "gz", gz, d))
    flat = [s.reshape(chunk_rows, width) for s in states]
    out = call(
        functools.partial(z_kernel, dims, [zc] * CHUNKS, gz),
        (
            project_in,
            project_out,
            norm_gains,
            expand_weight,
            reduce_weight,
            *flat,
            *normeds,
            *[t for per_shift in theirs for t in per_shift],
        ),
        shape((rows, width), F32),
        [
            pltpu.VMEM((width // LANES, rows, LANES), F32),
            pltpu.VMEM((gz, 2 * width // LANES, rows, LANES), F32),
            pltpu.VMEM((width // LANES, rows, LANES), F32),
            pltpu.VMEM((rows, width), BF16),
        ],
        20 * CHUNKS * cell,
    )
    return out.reshape(state_field.shape)


def solution(mesh):
    placed = (P("gx", "gy", "gz", None), P(), P(), P(), P(), P())
    sizes = tuple(mesh.shape[axis] for axis in ("gx", "gy", "gz"))

    def body(*args):
        return on_device(sizes, *args)

    return jax.shard_map(
        body, mesh=mesh, in_specs=placed, out_specs=P("gx", "gy", "gz", None), check_vma=False
    )
```
